512 devices in a mesh: ta: 32 (over y, x, core), sa: 16 (over z).
Axes of the slice: x: 4, y: 4, z: 16, core: 2. Of those that a mesh axis runs over, the one named last changes fastest.
Arguments:
- eigenvectors: bfloat16 [32, 256, 2, 3, 16, 384], P('ta', None, None, None, 'sa'), may hold values from -17 to 17
- momenta: int32 [8, 3], replicated, may hold values from -4 to 4
- block_order: int32 [4], replicated, may hold values from 0 to 3, each once
Outputs:
- meson_fields: float32 [8, 16, 64, 32, 128], P(None, 'sa', 'ta')
- slice_norms: float32 [32, 256], P('ta')
The draws below stay inside these ranges and needn't reach their ends.
Inputs may be any that keep to these rules, and one draw needn't show every extreme that they name: block_order names every block once.
All inputs are finite; a program needn't handle non-finite values.
Results may differ from the reference program's by a relative error of at most 0.0018.
Values sent between devices are 32-bit elements; how exact they have to be, the bound alone decides.
No kernel may reach another device: no remote copies, remote signals or barrier semaphores. Data moves between devices by JAX's collectives and lax.ppermute only.
A program may use at most 64 MiB of HBM per device.

```python
import math
import jax
import jax.numpy as jnp
from jax import lax

NC = 3
BS = 64
NBLK = 4
P_SIZE = 8
LX = 96
NV = 256
NT = 32
NZ = 16
PLANE = 384


def draw_eigenvectors(key, part):
    gauss_key, rough_key = jax.random.split(jax.random.fold_in(key, 17), 2)
    full_shape = (NT, NV, 2, NC, NZ, PLANE)
    roughness = jax.random.uniform(rough_key, (NT, 1, 1, 1, NZ, PLANE), jnp.float32, 0.7, 1.4)
    height = jnp.arange(NZ, dtype=jnp.float32) / max(NZ - 1, 1)
    rising = jnp.sqrt(1.0 + 2.0 * height).reshape(1, 1, 1, 1, NZ, 1)
    values = jnp.clip(jax.random.normal(gauss_key, full_shape, jnp.float32), -4.0, 4.0)
    return (values * roughness * rising).astype(jnp.bfloat16)


def place_ends(array, key, least, top_value):
    shape = array.shape
    index_at = [jax.random.randint(jax.random.fold_in(key, axis), (), 0, shape[axis]) for axis in range(len(shape))]
    array = array.at[tuple(index_at)].set(least)
    longest = shape.index(max(shape))
    index_at[longest] = (index_at[longest] + 1) % shape[longest]
    return array.at[tuple(index_at)].set(top_value)


def setup_inputs(seed: int = 0) -> dict:
    key_of = jax.random.split(jax.random.key(seed), 4)
    return {
        "eigenvectors": draw_eigenvectors(jax.random.fold_in(key_of[3], 71), 0),
        "momenta": place_ends(jax.random.randint(key_of[1], (P_SIZE, 3), -4, 5), jax.random.fold_in(key_of[1], 1), -4, 4).astype(jnp.int32),
        "block_order": jax.random.permutation(key_of[2], NBLK).astype(jnp.int32),
    }


full_turn = 2.0 * math.pi

def phased_right(blocks, cos_table, sin_table):
    real_part = blocks[:, :, 0].astype(jnp.float32)[None]
    imag_part = blocks[:, :, 1].astype(jnp.float32)[None]
    cos_full = cos_table[:, None, None, None, :]
    sin_full = sin_table[:, None, None, None, :]
    phased_re = (real_part * cos_full + imag_part * sin_full).astype(jnp.bfloat16)
    phased_im = (imag_part * cos_full - real_part * sin_full).astype(jnp.bfloat16)
    first_half = jnp.stack([phased_re, phased_im], axis=3)
    second_half = jnp.stack([phased_im, -phased_re], axis=3)
    right_cols = jnp.stack([first_half, second_half], axis=1)
    return right_cols.reshape(right_cols.shape[0], 2, right_cols.shape[2], right_cols.shape[3], -1)

def reference(eigenvectors, momenta, block_order):
    site_count = NZ * PLANE
    site_index = jnp.arange(site_count, dtype=jnp.int32)
    z_coord = site_index // PLANE
    within_plane = site_index % PLANE
    x_coord = within_plane % LX
    y_coord = within_plane // LX
    phase_index = momenta[:, 0:1] * x_coord[None, :] + momenta[:, 1:2] * y_coord[None, :] + momenta[:, 2:3] * z_coord[None, :]
    phase_index = jnp.mod(phase_index, LX).astype(jnp.int32)
    angles = phase_index.astype(jnp.float32) * (full_turn / LX)
    cosines = jnp.cos(angles)[:, None, :]
    sine_vals = jnp.sin(angles)[:, None, :]
    norm_scale = 1.0 / math.sqrt(2 * NC * NZ * PLANE)

    def one_slice(slab_data):
        blocks = slab_data.reshape(NBLK, BS, 2, NC, site_count)
        ordered = jnp.take(blocks, block_order, axis=0)
        left_rows = ordered.reshape(NBLK, BS, 2 * NC * site_count).astype(jnp.float32)

        def one_momentum(trig_pair):
            right_cols = phased_right(ordered, trig_pair[0], trig_pair[1])[0]
            product = jnp.einsum('ark,cbjk->abrcj', left_rows, right_cols.astype(jnp.float32))
            return product.reshape(NBLK * NBLK, BS, 2 * BS)
        fields = lax.map(one_momentum, (cosines, sine_vals))
        squares = lax.optimization_barrier(jnp.sum(jnp.square(slab_data.astype(jnp.float32)), axis=(1, 2, 3, 4)))
        return (fields, squares)
    fields, squares = lax.map(one_slice, eigenvectors)
    meson_fields = jnp.transpose(fields, (1, 2, 3, 0, 4)) * norm_scale
    slice_norms = squares / (2 * NC * NZ * PLANE)
    return (meson_fields, slice_norms)
```

```python
import math

import jax
import jax.numpy as jnp
from jax import lax
from jax.experimental import pallas as pl
from jax.experimental.pallas import tpu as pltpu
from jax.sharding import PartitionSpec as P

NC = 3
BS = 64
NBLK = 4
NV = NBLK * BS
LX = 96
PARTS = 2 * NC
full_turn = 2.0 * math.pi


def fields_kernel(planes, scale, order_ref, mom_ref, x_ref, out_ref, nrm_ref, left_ref, right_ref, cos_ref, sin_ref):
    p = pl.program_id(0)
    half = NC * planes

    @pl.when(p == 0)
    def _():
        site = lax.broadcasted_iota(jnp.int32, (mom_ref.shape[0], planes), 1).astype(jnp.float32)
        y = jnp.floor((site + 0.5) * (1.0 / LX))
        x = site - LX * y
        z = lax.axis_index("sa").astype(jnp.float32)
        mom = mom_ref[...].astype(jnp.float32)
        index = mom[:, 0:1] * x + mom[:, 1:2] * y + mom[:, 2:3] * z
        index = index - LX * jnp.floor((index + 0.5) * (1.0 / LX))
        angles = index * (full_turn / LX)
        cos_ref[...] = jnp.cos(angles)
        sin_ref[...] = jnp.sin(angles)
        for a in range(NBLK):
            rows = pl.ds(pl.multiple_of(order_ref[a] * BS, BS), BS)
            for c in range(NC):
                re = x_ref[c, rows, :]
                im = x_ref[NC + c, rows, :]
                lanes, after = pl.ds(c * planes, planes), pl.ds(half + c * planes, planes)
                left_ref[pl.ds(a * BS, BS), lanes] = re
                left_ref[pl.ds(a * BS, BS), after] = im
                left_ref[pl.ds(NV + a * BS, BS), lanes] = -im
                left_ref[pl.ds(NV + a * BS, BS), after] = re
        squares = jnp.zeros((NV, 128), jnp.float32)
        for k in range(PARTS):
            for l in range(planes // 128):
                v = x_ref[k, :, pl.ds(l * 128, 128)].astype(jnp.float32)
                squares = squares + v * v
        nrm_ref[...] = jnp.sum(squares.T, axis=0, keepdims=True)

    cos = cos_ref[pl.ds(p, 1), :]
    sin = sin_ref[pl.ds(p, 1), :]
    for c in range(NC):
        lanes, after = pl.ds(c * planes, planes), pl.ds(half + c * planes, planes)
        re = left_ref[pl.ds(0, NV), lanes].astype(jnp.float32)
        im = left_ref[pl.ds(0, NV), after].astype(jnp.float32)
        right_ref[:, lanes] = (re * cos + im * sin).astype(jnp.bfloat16)
        right_ref[:, after] = (im * cos - re * sin).astype(jnp.bfloat16)
    product = lax.dot_general(
        left_ref[...], right_ref[...], (((1,), (1,)), ((), ())), preferred_element_type=jnp.float32
    )
    product = product * scale
    low = lax.broadcasted_iota(jnp.int32, (NV, 128), 1) < BS
    for tile in range(NV // 128):
        real = product[:NV, tile * 128 : (tile + 1) * 128]
        imag = product[NV:, tile * 128 : (tile + 1) * 128]
        first = jnp.where(low, real, pltpu.roll(imag, BS, 1))
        second = jnp.where(low, pltpu.roll(real, BS, 1), imag)
        for a in range(NBLK):
            out_ref[a * NBLK + 2 * tile, 0] = first[a * BS : (a + 1) * BS]
            out_ref[a * NBLK + 2 * tile + 1, 0] = second[a * BS : (a + 1) * BS]


def partial_fields(parts, momenta, block_order, scale):
    planes = parts.shape[-1]
    momenta_count = momenta.shape[0]
    pairs = NBLK * NBLK
    return pl.pallas_call(
        lambda *refs: fields_kernel(planes, scale, *refs),
        grid=(momenta_count,),
        in_specs=[
            pl.BlockSpec(memory_space=pltpu.SMEM),
            pl.BlockSpec(memory_space=pltpu.VMEM),
            pl.BlockSpec(memory_space=pltpu.VMEM),
        ],
        out_specs=[
            pl.BlockSpec((pairs, 1, BS, 2 * BS), lambda p: (0, p, 0, 0)),
            pl.BlockSpec((1, NV), lambda p: (0, 0)),
        ],
        out_shape=[
            jax.ShapeDtypeStruct((pairs, momenta_count, BS, 2 * BS), jnp.float32),
            jax.ShapeDtypeStruct((1, NV), jnp.float32),
        ],
        scratch_shapes=[
            pltpu.VMEM((2 * NV, PARTS * planes), jnp.bfloat16),
            pltpu.VMEM((NV, PARTS * planes), jnp.bfloat16),
            pltpu.VMEM((momenta_count, planes), jnp.float32),
            pltpu.VMEM((momenta_count, planes), jnp.float32),
        ],
        compiler_params=pltpu.CompilerParams(vmem_limit_bytes=40 * 1024 * 1024),
        name="fields",
    )(block_order, momenta, parts)


def body(eigenvectors, momenta, block_order):
    planes = eigenvectors.shape[-1]
    entries = 2 * NC * lax.axis_size("sa") * planes
    parts = jnp.moveaxis(eigenvectors.reshape(NV, PARTS, planes), 1, 0)
    fields, local_sums = partial_fields(parts, momenta, block_order, 1.0 / math.sqrt(entries))
    count = momenta.shape[0]
    owned = lax.psum_scatter(
        fields.reshape(NBLK * NBLK, count * BS, 2 * BS), "sa", scatter_dimension=0, tiled=True
    )
    slice_norms = lax.psum(local_sums, "sa") / entries
    peers = lax.axis_size("ta")
    tiles = jnp.moveaxis(owned.reshape(count, peers, BS // peers, 2 * BS), 1, 0)
    tiles = lax.all_to_all(tiles, "ta", 0, 0, tiled=True)
    meson_fields = jnp.transpose(tiles, (1, 2, 0, 3))[:, None]
    return (meson_fields, slice_norms)


def solution(mesh):
    return jax.shard_map(
        body,
        mesh=mesh,
        in_specs=(P("ta", None, None, None, "sa", None), P(), P()),
        out_specs=(P(None, "sa", "ta", None, None), P("ta", None)),
        check_vma=False,
    )
```

```python
import math

import jax
import jax.numpy as jnp
from jax import lax
from jax.experimental import pallas as pl
from jax.experimental.pallas import tpu as pltpu
from jax.sharding import PartitionSpec as P

NC = 3
BS = 64
NBLK = 4
NV = NBLK * BS
LX = 96
PARTS = 2 * NC
full_turn = 2.0 * math.pi


def fields_kernel(planes, scale, order_ref, mom_ref, x_ref, out_ref, nrm_ref, left_ref, right_ref, cos_ref, sin_ref):
    p = pl.program_id(0)
    half = NC * planes

    @pl.when(p == 0)
    def _():
        site = lax.broadcasted_iota(jnp.int32, (mom_ref.shape[0], planes), 1).astype(jnp.float32)
        y = jnp.floor((site + 0.5) * (1.0 / LX))
        x = site - LX * y
        z = lax.axis_index("sa").astype(jnp.float32)
        mom = mom_ref[...].astype(jnp.float32)
        index = mom[:, 0:1] * x + mom[:, 1:2] * y + mom[:, 2:3] * z
        index = index - LX * jnp.floor((index + 0.5) * (1.0 / LX))
        angles = index * (full_turn / LX)
        cos_ref[...] = jnp.cos(angles)
        sin_ref[...] = jnp.sin(angles)
        for a in range(NBLK):
            rows = pl.ds(pl.multiple_of(order_ref[a] * BS, BS), BS)
            for c in range(NC):
                re = x_ref[c, rows, :]
                im = x_ref[NC + c, rows, :]
                lanes, after = pl.ds(c * planes, planes), pl.ds(half + c * planes, planes)
                left_ref[pl.ds(a * BS, BS), lanes] = re
                left_ref[pl.ds(a * BS, BS), after] = im
                left_ref[pl.ds(NV + a * BS, BS), lanes] = -im
                left_ref[pl.ds(NV + a * BS, BS), after] = re
        squares = jnp.zeros((NV, 128), jnp.float32)
        for k in range(PARTS):
            for l in range(planes // 128):
                v = x_ref[k, :, pl.ds(l * 128, 128)].astype(jnp.float32)
                squares = squares + v * v
        nrm_ref[...] = jnp.sum(squares.T, axis=0, keepdims=True)

    cos = cos_ref[pl.ds(p, 1), :]
    sin = sin_ref[pl.ds(p, 1), :]
    for c in range(NC):
        lanes, after = pl.ds(c * planes, planes), pl.ds(half + c * planes, planes)
        re = left_ref[pl.ds(0, NV), lanes].astype(jnp.float32)
        im = left_ref[pl.ds(0, NV), after].astype(jnp.float32)
        right_ref[:, lanes] = (re * cos + im * sin).astype(jnp.bfloat16)
        right_ref[:, after] = (im * cos - re * sin).astype(jnp.bfloat16)
    product = lax.dot_general(
        left_ref[...], right_ref[...], (((1,), (1,)), ((), ())), preferred_element_type=jnp.float32
    )
    product = product * scale
    low = lax.broadcasted_iota(jnp.int32, (NV, 128), 1) < BS
    for tile in range(NV // 128):
        real = product[:NV, tile * 128 : (tile + 1) * 128]
        imag = product[NV:, tile * 128 : (tile + 1) * 128]
        first = jnp.where(low, real, pltpu.roll(imag, BS, 1))
        second = jnp.where(low, pltpu.roll(real, BS, 1), imag)
        for a in range(NBLK):
            out_ref[a * NBLK + 2 * tile, 0] = first[a * BS : (a + 1) * BS]
            out_ref[a * NBLK + 2 * tile + 1, 0] = second[a * BS : (a + 1) * BS]


def partial_fields(parts, momenta, block_order, scale):
    planes = parts.shape[-1]
    momenta_count = momenta.shape[0]
    pairs = NBLK * NBLK
    return pl.pallas_call(
        lambda *refs: fields_kernel(planes, scale, *refs),
        grid=(momenta_count,),
        in_specs=[
            pl.BlockSpec(memory_space=pltpu.SMEM),
            pl.BlockSpec(memory_space=pltpu.VMEM),
            pl.BlockSpec(memory_space=pltpu.VMEM),
        ],
        out_specs=[
            pl.BlockSpec((pairs, 1, BS, 2 * BS), lambda p: (0, p, 0, 0)),
            pl.BlockSpec((1, NV), lambda p: (0, 0)),
        ],
        out_shape=[
            jax.ShapeDtypeStruct((pairs, momenta_count, BS, 2 * BS), jnp.float32),
            jax.ShapeDtypeStruct((1, NV), jnp.float32),
        ],
        scratch_shapes=[
            pltpu.VMEM((2 * NV, PARTS * planes), jnp.bfloat16),
            pltpu.VMEM((NV, PARTS * planes), jnp.bfloat16),
            pltpu.VMEM((momenta_count, planes), jnp.float32),
            pltpu.VMEM((momenta_count, planes), jnp.float32),
        ],
        compiler_params=pltpu.CompilerParams(vmem_limit_bytes=40 * 1024 * 1024),
        name="fields",
    )(block_order, momenta, parts)


def body(eigenvectors, momenta, block_order):
    planes = eigenvectors.shape[-1]
    entries = 2 * NC * lax.axis_size("sa") * planes
    parts = jnp.moveaxis(eigenvectors.reshape(NV, PARTS, planes), 1, 0)
    fields, local_sums = partial_fields(parts, momenta, block_order, 1.0 / math.sqrt(entries))
    count = momenta.shape[0]
    owned = lax.psum_scatter(
        fields.reshape(NBLK * NBLK, count * BS, 2 * BS), "sa", scatter_dimension=0, tiled=True
    )
    summed = lax.psum(local_sums, "sa")
    owned, summed = lax.optimization_barrier((owned, summed))
    peers = lax.axis_size("ta")
    tiles = jnp.moveaxis(owned.reshape(count, peers, BS // peers, 2 * BS), 1, 0)
    tiles = lax.all_to_all(tiles, "ta", 0, 0, tiled=True)
    meson_fields = jnp.transpose(tiles, (1, 2, 0, 3))[:, None]
    return (meson_fields, summed / entries)


def solution(mesh):
    return jax.shard_map(
        body,
        mesh=mesh,
        in_specs=(P("ta", None, None, None, "sa", None), P(), P()),
        out_specs=(P(None, "sa", "ta", None, None), P("ta", None)),
        check_vma=False,
    )
```

```python
import math

import jax
import jax.numpy as jnp
from jax import lax
from jax.experimental import pallas as pl
from jax.experimental.pallas import tpu as pltpu
from jax.sharding import PartitionSpec as P

NC = 3
BS = 64
NBLK = 4
NV = NBLK * BS
LX = 96
PARTS = 2 * NC
full_turn = 2.0 * math.pi


def fields_kernel(planes, scale, order_ref, mom_ref, x_ref, out_ref, nrm_ref, left_ref, right_ref, cos_ref, sin_ref):
    p = pl.program_id(0)
    half = NC * planes

    @pl.when(p == 0)
    def _():
        site = lax.broadcasted_iota(jnp.int32, (mom_ref.shape[0], planes), 1).astype(jnp.float32)
        y = jnp.floor((site + 0.5) * (1.0 / LX))
        x = site - LX * y
        z = lax.axis_index("sa").astype(jnp.float32)
        mom = mom_ref[...].astype(jnp.float32)
        index = mom[:, 0:1] * x + mom[:, 1:2] * y + mom[:, 2:3] * z
        index = index - LX * jnp.floor((index + 0.5) * (1.0 / LX))
        angles = index * (full_turn / LX)
        cos_ref[...] = jnp.cos(angles)
        sin_ref[...] = jnp.sin(angles)
        for a in range(NBLK):
            rows = pl.ds(pl.multiple_of(order_ref[a] * BS, BS), BS)
            for c in range(NC):
                re = x_ref[c, rows, :]
                im = x_ref[NC + c, rows, :]
                lanes, after = pl.ds(c * planes, planes), pl.ds(half + c * planes, planes)
                left_ref[pl.ds(a * BS, BS), lanes] = re
                left_ref[pl.ds(a * BS, BS), after] = im
                left_ref[pl.ds(NV + a * BS, BS), lanes] = -im
                left_ref[pl.ds(NV + a * BS, BS), after] = re
        squares = jnp.zeros((NV, 128), jnp.float32)
        for k in range(PARTS):
            for l in range(planes // 128):
                v = x_ref[k, :, pl.ds(l * 128, 128)].astype(jnp.float32)
                squares = squares + v * v
        nrm_ref[...] = jnp.sum(squares.T, axis=0, keepdims=True)

    cos = cos_ref[pl.ds(p, 1), :]
    sin = sin_ref[pl.ds(p, 1), :]
    for c in range(NC):
        lanes, after = pl.ds(c * planes, planes), pl.ds(half + c * planes, planes)
        re = left_ref[pl.ds(0, NV), lanes].astype(jnp.float32)
        im = left_ref[pl.ds(0, NV), after].astype(jnp.float32)
        right_ref[:, lanes] = (re * cos + im * sin).astype(jnp.bfloat16)
        right_ref[:, after] = (im * cos - re * sin).astype(jnp.bfloat16)
    product = lax.dot_general(
        left_ref[...], right_ref[...], (((1,), (1,)), ((), ())), preferred_element_type=jnp.float32
    )
    product = product * scale
    low = lax.broadcasted_iota(jnp.int32, (NV, 128), 1) < BS
    for tile in range(NV // 128):
        real = product[:NV, tile * 128 : (tile + 1) * 128]
        imag = product[NV:, tile * 128 : (tile + 1) * 128]
        first = jnp.where(low, real, pltpu.roll(imag, BS, 1))
        second = jnp.where(low, pltpu.roll(real, BS, 1), imag)
        for a in range(NBLK):
            out_ref[a * NBLK + 2 * tile, 0] = first[a * BS : (a + 1) * BS]
            out_ref[a * NBLK + 2 * tile + 1, 0] = second[a * BS : (a + 1) * BS]


def partial_fields(parts, momenta, block_order, scale):
    planes = parts.shape[-1]
    momenta_count = momenta.shape[0]
    pairs = NBLK * NBLK
    return pl.pallas_call(
        lambda *refs: fields_kernel(planes, scale, *refs),
        grid=(momenta_count,),
        in_specs=[
            pl.BlockSpec(memory_space=pltpu.SMEM),
            pl.BlockSpec(memory_space=pltpu.VMEM),
            pl.BlockSpec(memory_space=pltpu.VMEM),
        ],
        out_specs=[
            pl.BlockSpec((pairs, 1, BS, 2 * BS), lambda p: (0, p, 0, 0)),
            pl.BlockSpec((1, NV), lambda p: (0, 0)),
        ],
        out_shape=[
            jax.ShapeDtypeStruct((pairs, momenta_count, BS, 2 * BS), jnp.float32),
            jax.ShapeDtypeStruct((1, NV), jnp.float32),
        ],
        scratch_shapes=[
            pltpu.VMEM((2 * NV, PARTS * planes), jnp.bfloat16),
            pltpu.VMEM((NV, PARTS * planes), jnp.bfloat16),
            pltpu.VMEM((momenta_count, planes), jnp.float32),
            pltpu.VMEM((momenta_count, planes), jnp.float32),
        ],
        compiler_params=pltpu.CompilerParams(vmem_limit_bytes=40 * 1024 * 1024),
        name="fields",
    )(block_order, momenta, parts)


ROWS = 512
TAIL = 8


def add_kernel(first, toward, hop, nrm_ref, *refs):
    me = lax.axis_index("sa")
    peers = lax.axis_size("sa")
    if first:
        x_ref, g_ref, out_ref, g_out = refs
    else:
        x_ref, g_ref, got_ref, out_ref, g_out = refs
    owner = lax.rem(me + toward * (peers // 2 - hop) + (0 if toward > 0 else 1) + peers, peers)
    mine = x_ref[owner]
    if first:
        out_ref[pl.ds(0, ROWS)] = mine.reshape(ROWS, 128)
        out_ref[pl.ds(ROWS, TAIL)] = nrm_ref[...]
    else:
        out_ref[pl.ds(0, ROWS)] = mine.reshape(ROWS, 128) + got_ref[pl.ds(0, ROWS)]
        out_ref[pl.ds(ROWS, TAIL)] = got_ref[pl.ds(ROWS, TAIL)]
        g_out[hop - 1 + (0 if toward > 0 else 8)] = got_ref[pl.ds(ROWS, TAIL)]


def final_kernel(nrm_ref, x_ref, g_ref, r_ref, l_ref, out_ref, nsum_ref, slots):
    me = lax.axis_index("sa")
    peers = lax.axis_size("sa")
    for p in range(8):
        total = x_ref[me, p] + (r_ref[pl.ds(p * 64, 64)] + l_ref[pl.ds(p * 64, 64)])
        for r in range(32):
            out_ref[r, pl.ds(2 * p, 2)] = total[2 * r : 2 * r + 2]
    slots[me] = nrm_ref[...]
    for hop in range(8):
        slots[lax.rem(me - 1 - hop + peers, peers)] = r_ref[pl.ds(ROWS, TAIL)] if hop == 7 else g_ref[hop]
    for hop in range(7):
        slots[lax.rem(me + 1 + hop, peers)] = l_ref[pl.ds(ROWS, TAIL)] if hop == 6 else g_ref[8 + hop]
    total = slots[0]
    for k in range(1, 16):
        total = total + slots[k]
    nsum_ref[...] = total


def vm(n):
    return [pl.BlockSpec(memory_space=pltpu.VMEM)] * n


CP = pltpu.CompilerParams(vmem_limit_bytes=40 * 1024 * 1024)


def step(toward, hop, nrm, fields, g, got):
    first = got is None
    args = (nrm, fields, g) + (() if first else (got,))
    return pl.pallas_call(
        lambda *refs: add_kernel(first, toward, hop, *refs),
        in_specs=vm(len(args)),
        out_specs=vm(2),
        out_shape=[jax.ShapeDtypeStruct((ROWS + TAIL, 128), jnp.float32), jax.ShapeDtypeStruct((16, TAIL, 128), jnp.float32)],
        input_output_aliases={2: 1},
        compiler_params=CP,
        name="hop",
    )(*args)


def body(eigenvectors, momenta, block_order):
    planes = eigenvectors.shape[-1]
    n = lax.axis_size("sa")
    entries = 2 * NC * n * planes
    parts = jnp.moveaxis(eigenvectors.reshape(NV, PARTS, planes), 1, 0)
    fields, nrm = partial_fields(parts, momenta, block_order, 1.0 / math.sqrt(entries))
    nrm = jnp.pad(nrm.reshape(2, 128), ((0, 6), (0, 0)))
    up = [(i, (i + 1) % n) for i in range(n)]
    down = [(i, (i - 1) % n) for i in range(n)]
    g = jnp.zeros((16, TAIL, 128), jnp.float32)
    r = l = None
    for hop in range(8):
        send, g = step(1, hop, nrm, fields, g, r)
        r = lax.ppermute(send, "sa", up)
        if hop < 7:
            send, g = step(-1, hop, nrm, fields, g, l)
            l = lax.ppermute(send, "sa", down)
    tiles, nsum = pl.pallas_call(
        final_kernel,
        in_specs=vm(5),
        out_specs=vm(2),
        out_shape=[jax.ShapeDtypeStruct((32, 16, 128), jnp.float32), jax.ShapeDtypeStruct((TAIL, 128), jnp.float32)],
        scratch_shapes=[pltpu.VMEM((16, TAIL, 128), jnp.float32)],
        compiler_params=CP,
        name="final",
    )(nrm, fields, g, r, l)
    tiles = lax.all_to_all(tiles, "ta", 0, 0, tiled=True)
    meson_fields = jnp.transpose(tiles, (1, 0, 2)).reshape(8, 1, 2, 32, 128)
    return (meson_fields, nsum[:2].reshape(1, NV) / entries)


def solution(mesh):
    return jax.shard_map(
        body,
        mesh=mesh,
        in_specs=(P("ta", None, None, None, "sa", None), P(), P()),
        out_specs=(P(None, "sa", "ta", None, None), P("ta", None)),
        check_vma=False,
    )
```

```python
import math

import jax
import jax.numpy as jnp
from jax import lax
from jax.experimental import pallas as pl
from jax.experimental.pallas import tpu as pltpu
from jax.sharding import PartitionSpec as P

NC = 3
BS = 64
NBLK = 4
NV = NBLK * BS
LX = 96
PARTS = 2 * NC
full_turn = 2.0 * math.pi


def near_columns():
    first = lax.rem(lax.axis_index("sa") + lax.axis_size("sa") // 2, NBLK)
    columns = [lax.rem(first + k, NBLK) for k in range(NBLK)]
    return columns[:2], columns[2:]


def fill_left(order_ref, x_ref, left_ref):
    planes = x_ref.shape[-1]
    half = NC * planes
    for k in range(NBLK):
        stored = pl.ds(pl.multiple_of(order_ref[k] * BS, BS), BS)
        for c in range(NC):
            re = x_ref[c, stored, :]
            im = x_ref[NC + c, stored, :]
            lanes, after = pl.ds(c * planes, planes), pl.ds(half + c * planes, planes)
            left_ref[pl.ds(2 * k * BS, BS), lanes] = re
            left_ref[pl.ds(2 * k * BS, BS), after] = im
            left_ref[pl.ds((2 * k + 1) * BS, BS), lanes] = -im
            left_ref[pl.ds((2 * k + 1) * BS, BS), after] = re


def fill_right(n, b, count, order_ref, x_ref, cosines, sines, right_ref):
    planes = x_ref.shape[-1]
    half = NC * planes
    stored = pl.ds(pl.multiple_of(order_ref[b] * BS, BS), BS)
    for c in range(NC):
        re = x_ref[c, stored, :].astype(jnp.float32)
        im = x_ref[NC + c, stored, :].astype(jnp.float32)
        for p in range(count):
            cos = cosines[p : p + 1]
            sin = sines[p : p + 1]
            rows = pl.ds((n * count + p) * BS, BS)
            right_ref[rows, pl.ds(c * planes, planes)] = (re * cos + im * sin).astype(jnp.bfloat16)
            right_ref[rows, pl.ds(half + c * planes, planes)] = (im * cos - re * sin).astype(jnp.bfloat16)


def multiply(columns, scale, order_ref, x_ref, cosines, sines, right_ref, left_ref, out_ref):
    count = cosines.shape[0]
    size = count * BS
    for n, b in enumerate(columns):
        fill_right(n, b, count, order_ref, x_ref, cosines, sines, right_ref)
    product = lax.dot_general(
        right_ref[...], left_ref[...], (((1,), (1,)), ((), ())), preferred_element_type=jnp.float32
    )
    product = product * scale
    for n, b in enumerate(columns):
        for a in range(NBLK):
            cut = product[n * size : (n + 1) * size, a * 2 * BS : (a + 1) * 2 * BS]
            out_ref[a * NBLK + b] = cut.reshape(count, BS, 2 * BS)


def first_kernel(scale, order_ref, mom_ref, x_ref, out_ref, nrm_ref, left_ref, cos_ref, sin_ref, right_ref):
    planes = x_ref.shape[-1]
    count = mom_ref.shape[1]
    site = lax.broadcasted_iota(jnp.int32, (count, planes), 1).astype(jnp.float32)
    y = jnp.floor((site + 0.5) * (1.0 / LX))
    x = site - LX * y
    z = lax.axis_index("sa").astype(jnp.float32)
    which = lax.broadcasted_iota(jnp.int32, (count, planes), 0)
    mom = [jnp.zeros((count, planes), jnp.float32)] * 3
    for p in range(count):
        mom = [jnp.where(which == p, mom_ref[k, p].astype(jnp.float32), mom[k]) for k in range(3)]
    index = mom[0] * x + mom[1] * y + mom[2] * z
    index = index - LX * jnp.floor((index + 0.5) * (1.0 / LX))
    angles = index * (full_turn / LX)
    cosines = jnp.cos(angles)
    sines = jnp.sin(angles)
    cos_ref[...] = cosines
    sin_ref[...] = sines
    fill_left(order_ref, x_ref, left_ref)
    multiply(near_columns()[0], scale, order_ref, x_ref, cosines, sines, right_ref, left_ref, out_ref)
    squares = jnp.zeros((NV, 128), jnp.float32)
    for k in range(PARTS):
        for l in range(planes // 128):
            v = x_ref[k, :, pl.ds(l * 128, 128)].astype(jnp.float32)
            squares = squares + v * v
    sums = jnp.sum(squares.T, axis=0, keepdims=True)
    nrm_ref[...] = jnp.zeros(nrm_ref.shape, jnp.float32)
    for k in range(NV // 128):
        nrm_ref[pl.ds(k, 1)] = sums[:, k * 128 : (k + 1) * 128]


def second_kernel(scale, order_ref, x_ref, cos_ref, sin_ref, left_ref, made_ref, after_ref, out_ref, right_ref):
    multiply(near_columns()[1], scale, order_ref, x_ref, cos_ref[...], sin_ref[...], right_ref, left_ref, out_ref)


def first_half(parts, momenta, block_order, scale):
    planes = parts.shape[-1]
    count = momenta.shape[0]
    depth = PARTS * planes
    return pl.pallas_call(
        lambda *refs: first_kernel(scale, *refs),
        in_specs=[pl.BlockSpec(memory_space=pltpu.SMEM)] * 2 + vm(1),
        out_specs=vm(5),
        out_shape=[
            jax.ShapeDtypeStruct((NBLK * NBLK, count, BS, 2 * BS), jnp.float32),
            jax.ShapeDtypeStruct((TAIL, 128), jnp.float32),
            jax.ShapeDtypeStruct((2 * NV, depth), jnp.bfloat16),
            jax.ShapeDtypeStruct((count, planes), jnp.float32),
            jax.ShapeDtypeStruct((count, planes), jnp.float32),
        ],
        scratch_shapes=[pltpu.VMEM((count * 2 * BS, depth), jnp.bfloat16)],
        compiler_params=CP,
        name="fields_first",
    )(block_order, momenta.T, parts)


def second_half(parts, block_order, made, after, scale):
    fields, _, left, cosines, sines = made
    return pl.pallas_call(
        lambda *refs: second_kernel(scale, *refs),
        in_specs=[pl.BlockSpec(memory_space=pltpu.SMEM)] + vm(5) + [pl.BlockSpec(memory_space=pl.ANY)],
        out_specs=vm(1)[0],
        out_shape=jax.ShapeDtypeStruct(fields.shape, jnp.float32),
        input_output_aliases={5: 0},
        scratch_shapes=[pltpu.VMEM((cosines.shape[0] * 2 * BS, left.shape[1]), jnp.bfloat16)],
        compiler_params=CP,
        name="fields_second",
    )(block_order, parts, cosines, sines, left, fields, after)


ROWS = 512
TAIL = 8


def add_kernel(first, toward, hop, nrm_ref, *refs):
    me = lax.axis_index("sa")
    peers = lax.axis_size("sa")
    if first:
        x_ref, g_ref, out_ref, g_out = refs
    else:
        x_ref, g_ref, got_ref, out_ref, g_out = refs
    owner = lax.rem(me + toward * (peers // 2 - hop) + (0 if toward > 0 else 1) + peers, peers)
    mine = x_ref[owner]
    if first:
        out_ref[pl.ds(0, ROWS)] = mine.reshape(ROWS, 128)
        out_ref[pl.ds(ROWS, TAIL)] = nrm_ref[...]
    else:
        out_ref[pl.ds(0, ROWS)] = mine.reshape(ROWS, 128) + got_ref[pl.ds(0, ROWS)]
        out_ref[pl.ds(ROWS, TAIL)] = got_ref[pl.ds(ROWS, TAIL)]
        g_out[hop - 1 + (0 if toward > 0 else 8)] = got_ref[pl.ds(ROWS, TAIL)]


def final_kernel(entries, nrm_ref, x_ref, g_ref, r_ref, l_ref, out_ref, nsum_ref, slots):
    me = lax.axis_index("sa")
    peers = lax.axis_size("sa")
    low = lax.broadcasted_iota(jnp.int32, (BS, 2 * BS), 1) < BS
    for p in range(0, 8, 2):
        rows = pl.ds(p * BS, 2 * BS)
        total = x_ref[me, pl.ds(p, 2)].reshape(2 * BS, 2 * BS) + (r_ref[rows] + l_ref[rows])
        turned = total.T
        real, imag = turned[:BS], turned[BS:]
        for k, tile in enumerate(
            (jnp.where(low, real, pltpu.roll(imag, BS, 1)), jnp.where(low, pltpu.roll(real, BS, 1), imag))
        ):
            for r in range(32):
                out_ref[r, pl.ds(2 * (p + k), 2)] = tile[2 * r : 2 * r + 2]
    slots[me] = nrm_ref[...]
    for hop in range(8):
        slots[lax.rem(me - 1 - hop + peers, peers)] = r_ref[pl.ds(ROWS, TAIL)] if hop == 7 else g_ref[hop]
    for hop in range(7):
        slots[lax.rem(me + 1 + hop, peers)] = l_ref[pl.ds(ROWS, TAIL)] if hop == 6 else g_ref[8 + hop]
    total = slots[0]
    for k in range(1, 16):
        total = total + slots[k]
    for k in range(NV // 128):
        nsum_ref[:, pl.ds(k * 128, 128)] = total[k : k + 1] / entries


def vm(n):
    return [pl.BlockSpec(memory_space=pltpu.VMEM)] * n


CP = pltpu.CompilerParams(vmem_limit_bytes=40 * 1024 * 1024)


def step(toward, hop, nrm, fields, g, got):
    first = got is None
    args = (nrm, fields, g) + (() if first else (got,))
    return pl.pallas_call(
        lambda *refs: add_kernel(first, toward, hop, *refs),
        in_specs=vm(len(args)),
        out_specs=vm(2),
        out_shape=[jax.ShapeDtypeStruct((ROWS + TAIL, 128), jnp.float32), jax.ShapeDtypeStruct((16, TAIL, 128), jnp.float32)],
        input_output_aliases={2: 1},
        compiler_params=CP,
        name="hop",
    )(*args)


def body(eigenvectors, momenta, block_order):
    planes = eigenvectors.shape[-1]
    n = lax.axis_size("sa")
    entries = 2 * NC * n * planes
    parts = jnp.moveaxis(eigenvectors.reshape(NV, PARTS, planes), 1, 0)
    scale = 1.0 / math.sqrt(entries)
    made = first_half(parts, momenta, block_order, scale)
    fields, nrm = made[:2]
    up = [(i, (i + 1) % n) for i in range(n)]
    down = [(i, (i - 1) % n) for i in range(n)]
    g = jnp.zeros((16, TAIL, 128), jnp.float32)
    r = l = None
    for hop in range(8):
        send, g = step(1, hop, nrm, fields, g, r)
        r = lax.ppermute(send, "sa", up)
        if hop < 7:
            send, g = step(-1, hop, nrm, fields, g, l)
            l = lax.ppermute(send, "sa", down)
        if hop == 0:
            fields = second_half(parts, block_order, made, g, scale)
    tiles, nsum = pl.pallas_call(
        lambda *refs: final_kernel(entries, *refs),
        in_specs=vm(5),
        out_specs=vm(2),
        out_shape=[jax.ShapeDtypeStruct((32, 16, 128), jnp.float32), jax.ShapeDtypeStruct((1, NV), jnp.float32)],
        scratch_shapes=[pltpu.VMEM((16, TAIL, 128), jnp.float32)],
        compiler_params=CP,
        name="final",
    )(nrm, fields, g, r, l)
    tiles = lax.all_to_all(tiles, "ta", 0, 0, tiled=True)
    meson_fields = jnp.transpose(tiles, (1, 0, 2)).reshape(8, 1, 2, 32, 128)
    return (meson_fields, nsum)


def solution(mesh):
    return jax.shard_map(
        body,
        mesh=mesh,
        in_specs=(P("ta", None, None, None, "sa", None), P(), P()),
        out_specs=(P(None, "sa", "ta", None, None), P("ta", None)),
        check_vma=False,
    )
```

```python
import math

import jax
import jax.numpy as jnp
from jax import lax
from jax.experimental import pallas as pl
from jax.experimental.pallas import tpu as pltpu
from jax.sharding import PartitionSpec as P

NC = 3
BS = 64
NBLK = 4
NV = NBLK * BS
LX = 96
PARTS = 2 * NC
full_turn = 2.0 * math.pi


def near_columns():
    first = lax.rem(lax.axis_index("sa") + lax.axis_size("sa") // 2, NBLK)
    columns = [lax.rem(first + k, NBLK) for k in range(NBLK)]
    return columns[:2], columns[2:]


def fill_left(order_ref, x_ref, left_ref):
    planes = x_ref.shape[-1]
    half = NC * planes
    for k in range(NBLK):
        stored = pl.ds(pl.multiple_of(order_ref[k] * BS, BS), BS)
        for c in range(NC):
            re = x_ref[c, stored, :]
            im = x_ref[NC + c, stored, :]
            lanes, after = pl.ds(c * planes, planes), pl.ds(half + c * planes, planes)
            left_ref[pl.ds(2 * k * BS, BS), lanes] = re
            left_ref[pl.ds(2 * k * BS, BS), after] = im
            left_ref[pl.ds((2 * k + 1) * BS, BS), lanes] = -im
            left_ref[pl.ds((2 * k + 1) * BS, BS), after] = re


def fill_right(n, b, left_ref, cosines, sines, right_ref):
    count, planes = cosines.shape
    half = NC * planes
    held = pl.ds(pl.multiple_of(b * 2 * BS, 2 * BS), BS)
    for c in range(NC):
        lanes, after = pl.ds(c * planes, planes), pl.ds(half + c * planes, planes)
        re = left_ref[held, lanes].astype(jnp.float32)
        im = left_ref[held, after].astype(jnp.float32)
        for p in range(count):
            cos = cosines[p : p + 1]
            sin = sines[p : p + 1]
            rows = pl.ds((n * count + p) * BS, BS)
            right_ref[rows, lanes] = (re * cos + im * sin).astype(jnp.bfloat16)
            right_ref[rows, after] = (im * cos - re * sin).astype(jnp.bfloat16)


def multiply(columns, scale, cosines, sines, right_ref, left_ref, out_ref):
    count = cosines.shape[0]
    size = count * BS
    for n, b in enumerate(columns):
        fill_right(n, b, left_ref, cosines, sines, right_ref)
    product = lax.dot_general(
        right_ref[...], left_ref[...], (((1,), (1,)), ((), ())), preferred_element_type=jnp.float32
    )
    product = product * scale
    for n, b in enumerate(columns):
        for a in range(NBLK):
            cut = product[n * size : (n + 1) * size, a * 2 * BS : (a + 1) * 2 * BS]
            out_ref[a * NBLK + b] = cut.reshape(count, BS, 2 * BS)


def first_kernel(scale, order_ref, mom_ref, x_ref, out_ref, nrm_ref, left_ref, cos_ref, sin_ref, right_ref):
    planes = x_ref.shape[-1]
    count = mom_ref.shape[1]
    site = lax.broadcasted_iota(jnp.int32, (count, planes), 1).astype(jnp.float32)
    y = jnp.floor((site + 0.5) * (1.0 / LX))
    x = site - LX * y
    z = lax.axis_index("sa").astype(jnp.float32)
    which = lax.broadcasted_iota(jnp.int32, (count, planes), 0)
    mom = [jnp.zeros((count, planes), jnp.float32)] * 3
    for p in range(count):
        mom = [jnp.where(which == p, mom_ref[k, p].astype(jnp.float32), mom[k]) for k in range(3)]
    index = mom[0] * x + mom[1] * y + mom[2] * z
    index = index - LX * jnp.floor((index + 0.5) * (1.0 / LX))
    angles = index * (full_turn / LX)
    cosines = jnp.cos(angles)
    sines = jnp.sin(angles)
    cos_ref[...] = cosines
    sin_ref[...] = sines
    fill_left(order_ref, x_ref, left_ref)
    multiply(near_columns()[0], scale, cosines, sines, right_ref, left_ref, out_ref)
    squares = jnp.zeros((NV, 128), jnp.float32)
    for k in range(PARTS):
        for l in range(planes // 128):
            v = x_ref[k, :, pl.ds(l * 128, 128)].astype(jnp.float32)
            squares = squares + v * v
    sums = jnp.sum(squares.T, axis=0, keepdims=True)
    nrm_ref[...] = jnp.zeros(nrm_ref.shape, jnp.float32)
    for k in range(NV // 128):
        nrm_ref[pl.ds(k, 1)] = sums[:, k * 128 : (k + 1) * 128]


def second_kernel(scale, order_ref, x_ref, cos_ref, sin_ref, left_ref, made_ref, after_ref, out_ref, right_ref):
    multiply(near_columns()[1], scale, cos_ref[...], sin_ref[...], right_ref, left_ref, out_ref)


def first_half(parts, momenta, block_order, scale):
    planes = parts.shape[-1]
    count = momenta.shape[0]
    depth = PARTS * planes
    return pl.pallas_call(
        lambda *refs: first_kernel(scale, *refs),
        in_specs=[pl.BlockSpec(memory_space=pltpu.SMEM)] * 2 + vm(1),
        out_specs=vm(5),
        out_shape=[
            jax.ShapeDtypeStruct((NBLK * NBLK, count, BS, 2 * BS), jnp.float32),
            jax.ShapeDtypeStruct((TAIL, 128), jnp.float32),
            jax.ShapeDtypeStruct((2 * NV, depth), jnp.bfloat16),
            jax.ShapeDtypeStruct((count, planes), jnp.float32),
            jax.ShapeDtypeStruct((count, planes), jnp.float32),
        ],
        scratch_shapes=[pltpu.VMEM((count * 2 * BS, depth), jnp.bfloat16)],
        compiler_params=CP,
        name="fields_first",
    )(block_order, momenta.T, parts)


def second_half(parts, block_order, made, after, scale):
    fields, _, left, cosines, sines = made
    return pl.pallas_call(
        lambda *refs: second_kernel(scale, *refs),
        in_specs=[pl.BlockSpec(memory_space=pltpu.SMEM)] + vm(5) + [pl.BlockSpec(memory_space=pl.ANY)],
        out_specs=vm(1)[0],
        out_shape=jax.ShapeDtypeStruct(fields.shape, jnp.float32),
        input_output_aliases={5: 0},
        scratch_shapes=[pltpu.VMEM((cosines.shape[0] * 2 * BS, left.shape[1]), jnp.bfloat16)],
        compiler_params=CP,
        name="fields_second",
    )(block_order, parts, cosines, sines, left, fields, after)


ROWS = 512
TAIL = 8


def add_kernel(first, toward, hop, nrm_ref, *refs):
    me = lax.axis_index("sa")
    peers = lax.axis_size("sa")
    if first:
        x_ref, g_ref, out_ref, g_out = refs
    else:
        x_ref, g_ref, got_ref, out_ref, g_out = refs
    owner = lax.rem(me + toward * (peers // 2 - hop) + (0 if toward > 0 else 1) + peers, peers)
    mine = x_ref[owner]
    if first:
        out_ref[pl.ds(0, ROWS)] = mine.reshape(ROWS, 128)
        out_ref[pl.ds(ROWS, TAIL)] = nrm_ref[...]
    else:
        out_ref[pl.ds(0, ROWS)] = mine.reshape(ROWS, 128) + got_ref[pl.ds(0, ROWS)]
        out_ref[pl.ds(ROWS, TAIL)] = got_ref[pl.ds(ROWS, TAIL)]
        g_out[hop - 1 + (0 if toward > 0 else 8)] = got_ref[pl.ds(ROWS, TAIL)]


def final_kernel(entries, nrm_ref, x_ref, g_ref, r_ref, l_ref, out_ref, nsum_ref, slots):
    me = lax.axis_index("sa")
    peers = lax.axis_size("sa")
    low = lax.broadcasted_iota(jnp.int32, (BS, 2 * BS), 1) < BS
    for p in range(0, 8, 2):
        rows = pl.ds(p * BS, 2 * BS)
        total = x_ref[me, pl.ds(p, 2)].reshape(2 * BS, 2 * BS) + (r_ref[rows] + l_ref[rows])
        turned = total.T
        real, imag = turned[:BS], turned[BS:]
        for k, tile in enumerate(
            (jnp.where(low, real, pltpu.roll(imag, BS, 1)), jnp.where(low, pltpu.roll(real, BS, 1), imag))
        ):
            for r in range(32):
                out_ref[r, pl.ds(2 * (p + k), 2)] = tile[2 * r : 2 * r + 2]
    slots[me] = nrm_ref[...]
    for hop in range(8):
        slots[lax.rem(me - 1 - hop + peers, peers)] = r_ref[pl.ds(ROWS, TAIL)] if hop == 7 else g_ref[hop]
    for hop in range(7):
        slots[lax.rem(me + 1 + hop, peers)] = l_ref[pl.ds(ROWS, TAIL)] if hop == 6 else g_ref[8 + hop]
    total = slots[0]
    for k in range(1, 16):
        total = total + slots[k]
    for k in range(NV // 128):
        nsum_ref[:, pl.ds(k * 128, 128)] = total[k : k + 1] / entries


def vm(n):
    return [pl.BlockSpec(memory_space=pltpu.VMEM)] * n


CP = pltpu.CompilerParams(vmem_limit_bytes=40 * 1024 * 1024)


def step(toward, hop, nrm, fields, g, got):
    first = got is None
    args = (nrm, fields, g) + (() if first else (got,))
    return pl.pallas_call(
        lambda *refs: add_kernel(first, toward, hop, *refs),
        in_specs=vm(len(args)),
        out_specs=vm(2),
        out_shape=[jax.ShapeDtypeStruct((ROWS + TAIL, 128), jnp.float32), jax.ShapeDtypeStruct((16, TAIL, 128), jnp.float32)],
        input_output_aliases={2: 1},
        compiler_params=CP,
        name="hop",
    )(*args)


def body(eigenvectors, momenta, block_order):
    planes = eigenvectors.shape[-1]
    n = lax.axis_size("sa")
    entries = 2 * NC * n * planes
    parts = jnp.moveaxis(eigenvectors.reshape(NV, PARTS, planes), 1, 0)
    scale = 1.0 / math.sqrt(entries)
    made = first_half(parts, momenta, block_order, scale)
    fields, nrm = made[:2]
    up = [(i, (i + 1) % n) for i in range(n)]
    down = [(i, (i - 1) % n) for i in range(n)]
    g = jnp.zeros((16, TAIL, 128), jnp.float32)
    r = l = None
    for hop in range(8):
        send, g = step(1, hop, nrm, fields, g, r)
        r = lax.ppermute(send, "sa", up)
        if hop < 7:
            send, g = step(-1, hop, nrm, fields, g, l)
            l = lax.ppermute(send, "sa", down)
        if hop == 0:
            fields = second_half(parts, block_order, made, g, scale)
    tiles, nsum = pl.pallas_call(
        lambda *refs: final_kernel(entries, *refs),
        in_specs=vm(5),
        out_specs=vm(2),
        out_shape=[jax.ShapeDtypeStruct((32, 16, 128), jnp.float32), jax.ShapeDtypeStruct((1, NV), jnp.float32)],
        scratch_shapes=[pltpu.VMEM((16, TAIL, 128), jnp.float32)],
        compiler_params=CP,
        name="final",
    )(nrm, fields, g, r, l)
    tiles = lax.all_to_all(tiles, "ta", 0, 0, tiled=True)
    meson_fields = jnp.transpose(tiles, (1, 0, 2)).reshape(8, 1, 2, 32, 128)
    return (meson_fields, nsum)


def solution(mesh):
    return jax.shard_map(
        body,
        mesh=mesh,
        in_specs=(P("ta", None, None, None, "sa", None), P(), P()),
        out_specs=(P(None, "sa", "ta", None, None), P("ta", None)),
        check_vma=False,
    )
```

```python
import math

import jax
import jax.numpy as jnp
from jax import lax
from jax.experimental import pallas as pl
from jax.experimental.pallas import tpu as pltpu
from jax.sharding import PartitionSpec as P

NC = 3
BS = 64
NBLK = 4
NV = NBLK * BS
LX = 96
PARTS = 2 * NC
full_turn = 2.0 * math.pi


def near_columns():
    first = lax.rem(lax.axis_index("sa") + lax.axis_size("sa") // 2, NBLK)
    columns = [lax.rem(first + k, NBLK) for k in range(NBLK)]
    return columns


def fill_left(order_ref, x_ref, left_ref):
    planes = x_ref.shape[-1]
    half = NC * planes
    for k in range(NBLK):
        stored = pl.ds(pl.multiple_of(order_ref[k] * BS, BS), BS)
        for c in range(NC):
            re = x_ref[c, stored, :]
            im = x_ref[NC + c, stored, :]
            lanes, after = pl.ds(c * planes, planes), pl.ds(half + c * planes, planes)
            left_ref[pl.ds(2 * k * BS, BS), lanes] = re
            left_ref[pl.ds(2 * k * BS, BS), after] = im
            left_ref[pl.ds((2 * k + 1) * BS, BS), lanes] = -im
            left_ref[pl.ds((2 * k + 1) * BS, BS), after] = re


def fill_right(n, b, left_ref, cosines, sines, right_ref):
    count, planes = cosines.shape
    half = NC * planes
    held = pl.ds(pl.multiple_of(b * 2 * BS, 2 * BS), BS)
    for c in range(NC):
        lanes, after = pl.ds(c * planes, planes), pl.ds(half + c * planes, planes)
        re = left_ref[held, lanes].astype(jnp.float32)
        im = left_ref[held, after].astype(jnp.float32)
        for p in range(count):
            cos = cosines[p : p + 1]
            sin = sines[p : p + 1]
            rows = pl.ds((n * count + p) * BS, BS)
            right_ref[rows, lanes] = (re * cos + im * sin).astype(jnp.bfloat16)
            right_ref[rows, after] = (im * cos - re * sin).astype(jnp.bfloat16)


def multiply(columns, scale, cosines, sines, right_ref, left_ref, out_ref):
    count = cosines.shape[0]
    size = count * BS
    for n, b in enumerate(columns):
        fill_right(n, b, left_ref, cosines, sines, right_ref)
    product = lax.dot_general(
        right_ref[...], left_ref[...], (((1,), (1,)), ((), ())), preferred_element_type=jnp.float32
    )
    product = product * scale
    for n, b in enumerate(columns):
        for a in range(NBLK):
            cut = product[n * size : (n + 1) * size, a * 2 * BS : (a + 1) * 2 * BS]
            out_ref[a * NBLK + b] = cut.reshape(count, BS, 2 * BS)


def first_kernel(scale, order_ref, mom_ref, x_ref, out_ref, nrm_ref, left_ref, cos_ref, sin_ref, right_ref):
    planes = x_ref.shape[-1]
    count = mom_ref.shape[1]
    site = lax.broadcasted_iota(jnp.int32, (count, planes), 1).astype(jnp.float32)
    y = jnp.floor((site + 0.5) * (1.0 / LX))
    x = site - LX * y
    z = lax.axis_index("sa").astype(jnp.float32)
    which = lax.broadcasted_iota(jnp.int32, (count, planes), 0)
    mom = [jnp.zeros((count, planes), jnp.float32)] * 3
    for p in range(count):
        mom = [jnp.where(which == p, mom_ref[k, p].astype(jnp.float32), mom[k]) for k in range(3)]
    index = mom[0] * x + mom[1] * y + mom[2] * z
    index = index - LX * jnp.floor((index + 0.5) * (1.0 / LX))
    angles = index * (full_turn / LX)
    cosines = jnp.cos(angles)
    sines = jnp.sin(angles)
    cos_ref[...] = cosines
    sin_ref[...] = sines
    fill_left(order_ref, x_ref, left_ref)
    multiply(near_columns()[:1], scale, cosines, sines, right_ref, left_ref, out_ref)
    squares = jnp.zeros((NV, 128), jnp.float32)
    for k in range(PARTS):
        for l in range(planes // 128):
            v = x_ref[k, :, pl.ds(l * 128, 128)].astype(jnp.float32)
            squares = squares + v * v
    sums = jnp.sum(squares.T, axis=0, keepdims=True)
    nrm_ref[...] = jnp.zeros(nrm_ref.shape, jnp.float32)
    for k in range(NV // 128):
        nrm_ref[pl.ds(k, 1)] = sums[:, k * 128 : (k + 1) * 128]


def more_kernel(cut, scale, cos_ref, sin_ref, left_ref, made_ref, after_ref, out_ref, right_ref):
    multiply(near_columns()[cut], scale, cos_ref[...], sin_ref[...], right_ref, left_ref, out_ref)


def first_half(parts, momenta, block_order, scale):
    planes = parts.shape[-1]
    count = momenta.shape[0]
    depth = PARTS * planes
    return pl.pallas_call(
        lambda *refs: first_kernel(scale, *refs),
        in_specs=[pl.BlockSpec(memory_space=pltpu.SMEM)] * 2 + vm(1),
        out_specs=vm(5),
        out_shape=[
            jax.ShapeDtypeStruct((NBLK * NBLK, count, BS, 2 * BS), jnp.float32),
            jax.ShapeDtypeStruct((TAIL, 128), jnp.float32),
            jax.ShapeDtypeStruct((2 * NV, depth), jnp.bfloat16),
            jax.ShapeDtypeStruct((count, planes), jnp.float32),
            jax.ShapeDtypeStruct((count, planes), jnp.float32),
        ],
        scratch_shapes=[pltpu.VMEM((count * BS, depth), jnp.bfloat16)],
        compiler_params=CP,
        name="fields_first",
    )(block_order, momenta.T, parts)


def more_columns(cut, made, fields, after, scale):
    _, _, left, cosines, sines = made
    columns = cut.stop - cut.start
    return pl.pallas_call(
        lambda *refs: more_kernel(cut, scale, *refs),
        in_specs=vm(4) + [pl.BlockSpec(memory_space=pl.ANY)],
        out_specs=vm(1)[0],
        out_shape=jax.ShapeDtypeStruct(fields.shape, jnp.float32),
        input_output_aliases={3: 0},
        scratch_shapes=[pltpu.VMEM((cosines.shape[0] * columns * BS, left.shape[1]), jnp.bfloat16)],
        compiler_params=CP,
        name="fields_more",
    )(cosines, sines, left, fields, after)


ROWS = 512
TAIL = 8


def add_kernel(first, toward, hop, nrm_ref, *refs):
    me = lax.axis_index("sa")
    peers = lax.axis_size("sa")
    if first:
        x_ref, g_ref, out_ref, g_out = refs
    else:
        x_ref, g_ref, got_ref, out_ref, g_out = refs
    owner = lax.rem(me + toward * (peers // 2 - hop) + (0 if toward > 0 else 1) + peers, peers)
    mine = x_ref[owner]
    if first:
        out_ref[pl.ds(0, ROWS)] = mine.reshape(ROWS, 128)
        out_ref[pl.ds(ROWS, TAIL)] = nrm_ref[...]
    else:
        out_ref[pl.ds(0, ROWS)] = mine.reshape(ROWS, 128) + got_ref[pl.ds(0, ROWS)]
        out_ref[pl.ds(ROWS, TAIL)] = got_ref[pl.ds(ROWS, TAIL)]
        g_out[hop - 1 + (0 if toward > 0 else 8)] = got_ref[pl.ds(ROWS, TAIL)]


def final_kernel(entries, nrm_ref, x_ref, g_ref, r_ref, l_ref, out_ref, nsum_ref, slots):
    me = lax.axis_index("sa")
    peers = lax.axis_size("sa")
    low = lax.broadcasted_iota(jnp.int32, (BS, 2 * BS), 1) < BS
    for p in range(0, 8, 2):
        rows = pl.ds(p * BS, 2 * BS)
        total = x_ref[me, pl.ds(p, 2)].reshape(2 * BS, 2 * BS) + (r_ref[rows] + l_ref[rows])
        turned = total.T
        real, imag = turned[:BS], turned[BS:]
        for k, tile in enumerate(
            (jnp.where(low, real, pltpu.roll(imag, BS, 1)), jnp.where(low, pltpu.roll(real, BS, 1), imag))
        ):
            for r in range(32):
                out_ref[r, pl.ds(2 * (p + k), 2)] = tile[2 * r : 2 * r + 2]
    slots[me] = nrm_ref[...]
    for hop in range(8):
        slots[lax.rem(me - 1 - hop + peers, peers)] = r_ref[pl.ds(ROWS, TAIL)] if hop == 7 else g_ref[hop]
    for hop in range(7):
        slots[lax.rem(me + 1 + hop, peers)] = l_ref[pl.ds(ROWS, TAIL)] if hop == 6 else g_ref[8 + hop]
    total = slots[0]
    for k in range(1, 16):
        total = total + slots[k]
    for k in range(NV // 128):
        nsum_ref[:, pl.ds(k * 128, 128)] = total[k : k + 1] / entries


def vm(n):
    return [pl.BlockSpec(memory_space=pltpu.VMEM)] * n


CP = pltpu.CompilerParams(vmem_limit_bytes=40 * 1024 * 1024)


def step(toward, hop, nrm, fields, g, got):
    first = got is None
    args = (nrm, fields, g) + (() if first else (got,))
    return pl.pallas_call(
        lambda *refs: add_kernel(first, toward, hop, *refs),
        in_specs=vm(len(args)),
        out_specs=vm(2),
        out_shape=[jax.ShapeDtypeStruct((ROWS + TAIL, 128), jnp.float32), jax.ShapeDtypeStruct((16, TAIL, 128), jnp.float32)],
        input_output_aliases={2: 1},
        compiler_params=CP,
        name="hop",
    )(*args)


def body(eigenvectors, momenta, block_order):
    planes = eigenvectors.shape[-1]
    n = lax.axis_size("sa")
    entries = 2 * NC * n * planes
    parts = jnp.moveaxis(eigenvectors.reshape(NV, PARTS, planes), 1, 0)
    scale = 1.0 / math.sqrt(entries)
    made = first_half(parts, momenta, block_order, scale)
    fields, nrm = made[:2]
    up = [(i, (i + 1) % n) for i in range(n)]
    down = [(i, (i - 1) % n) for i in range(n)]
    g = jnp.zeros((16, TAIL, 128), jnp.float32)
    r = l = None
    for hop in range(8):
        send, g = step(1, hop, nrm, fields, g, r)
        r = lax.ppermute(send, "sa", up)
        if hop == 0:
            fields = more_columns(slice(1, 2), made, fields, g, scale)
        if hop == 1:
            fields = more_columns(slice(2, 3), made, fields, g, scale)
        if hop < 7:
            send, g = step(-1, hop, nrm, fields, g, l)
            l = lax.ppermute(send, "sa", down)
        if hop == 0:
            fields = more_columns(slice(3, 4), made, fields, g, scale)
    tiles, nsum = pl.pallas_call(
        lambda *refs: final_kernel(entries, *refs),
        in_specs=vm(5),
        out_specs=vm(2),
        out_shape=[jax.ShapeDtypeStruct((32, 16, 128), jnp.float32), jax.ShapeDtypeStruct((1, NV), jnp.float32)],
        scratch_shapes=[pltpu.VMEM((16, TAIL, 128), jnp.float32)],
        compiler_params=CP,
        name="final",
    )(nrm, fields, g, r, l)
    tiles = lax.all_to_all(tiles, "ta", 0, 0, tiled=True)
    meson_fields = jnp.transpose(tiles, (1, 0, 2)).reshape(8, 1, 2, 32, 128)
    return (meson_fields, nsum)


def solution(mesh):
    return jax.shard_map(
        body,
        mesh=mesh,
        in_specs=(P("ta", None, None, None, "sa", None), P(), P()),
        out_specs=(P(None, "sa", "ta", None, None), P("ta", None)),
        check_vma=False,
    )
```
